512 devices in a mesh: dp: 8 (over y, core), rot: 64 (over z, x).
Axes of the slice: x: 4, y: 4, z: 16, core: 2. Of those that a mesh axis runs over, the one named last changes fastest.
Arguments:
- frames: int32 [128, 128, 512], P('dp'), may hold values from 0 to 8, as said below
- slices: float32 [128, 128, 512], P('rot'), may hold values from 0.125 to 8, as said below
Outputs:
- log_resp: float32 [128, 128, 512], P('dp', 'rot')
- new_slices: float32 [128, 128, 512], P('rot', 'dp')
The draws below stay inside these ranges and needn't reach their ends.
Inputs may be any that keep to these rules, and one draw needn't show every extreme that they name: `frames`: photon counts; each frame has its own brightness level. `slices`: positive intensities.
All inputs are finite; a program needn't handle non-finite values.
Results may differ from the reference program's by a relative error of at most 0.0012.
Values sent between devices are 32-bit elements; how exact they have to be, the bound alone decides.
A program may use at most 64 MiB of HBM per device.

```python
import math
import jax
import jax.numpy as jnp
from jax import lax

R = 128
PHI = 512
FRAMES = 128
TILTS = 128


def draw_frames(key, part):
    first, second = jax.random.split(jax.random.fold_in(key, 11))
    levels = jax.random.randint(first, (FRAMES, 1, 1), 1, 9)
    levels = jnp.where(jnp.arange(FRAMES)[:, None, None] == 0, 8, levels)
    raw = jax.random.randint(second, (FRAMES, R, PHI), 0, 1 << 20)
    return (raw % (levels + 1)).astype(jnp.int32)


def draw_slices(key, part):
    first = jax.random.fold_in(jax.random.fold_in(key, 23), 0)
    base = jnp.exp(jax.random.uniform(first, (TILTS, R, PHI), jnp.float32, -jnp.log(2.0), jnp.log(2.0)))
    return base.astype(jnp.float32)


def setup_inputs(seed: int = 0) -> dict:
    key_list = jax.random.split(jax.random.key(seed), 3)
    frames = draw_frames(jax.random.fold_in(key_list[2], 71), 0)
    slices = draw_slices(jax.random.fold_in(key_list[2], 71), 0)
    return dict(frames=frames, slices=slices)


HIGH = lax.Precision.HIGHEST

def angle_tables(length):
    index = jnp.arange(length, dtype=jnp.int32)
    phase = index[:, None] * index[None, :] % length
    radians = phase.astype(jnp.float32) * (2.0 * math.pi / length)
    return (jnp.cos(radians), jnp.sin(radians))

def spectral_cross_terms(left_re, left_im, right_re, right_im, form):
    real_part = jnp.einsum(form, left_re, right_re, precision=HIGH) + jnp.einsum(form, left_im, right_im, precision=HIGH)
    imag_part = jnp.einsum(form, left_im, right_re, precision=HIGH) - jnp.einsum(form, left_re, right_im, precision=HIGH)
    return jnp.concatenate([real_part, imag_part], axis=-1)

def reference(frames, slices):
    frame_count, shells, angles = frames.shape
    tilt_count = slices.shape[0]
    cosine, sine = angle_tables(angles)
    forward = jnp.concatenate([cosine, -sine], axis=1)
    inverse = jnp.concatenate([cosine, -sine], axis=0) / angles
    counts = frames.astype(jnp.bfloat16)
    frame_spec = jnp.dot(counts.reshape(-1, angles), forward.astype(jnp.bfloat16), preferred_element_type=jnp.float32)
    frame_spec = frame_spec.reshape(frame_count, shells, 2 * angles)
    model_spec = jnp.dot(jnp.log(slices).reshape(-1, angles), forward, precision=HIGH)
    model_spec = model_spec.reshape(tilt_count, shells, 2 * angles)
    frame_real, frame_imaginary = (frame_spec[..., :angles], frame_spec[..., angles:])
    model_real, model_imaginary = (model_spec[..., :angles], model_spec[..., angles:])
    cross_product = spectral_cross_terms(frame_real, frame_imaginary, model_real, model_imaginary, 'wlg,ilg->wig')
    corr = jnp.dot(cross_product.reshape(-1, 2 * angles), inverse, precision=HIGH).reshape(frame_count, tilt_count, angles)
    totals = lax.optimization_barrier(jnp.sum(slices, axis=(1, 2)))
    anneal = 4.0 / math.sqrt(shells * angles)
    scores = anneal * (corr - totals[None, :, None])
    top = lax.optimization_barrier(jnp.max(scores, axis=(1, 2)))
    lse = top + jnp.log(lax.optimization_barrier(jnp.sum(jnp.exp(scores - top[:, None, None]), axis=(1, 2))))
    log_resp = scores - lse[:, None, None]
    resp = jnp.exp(log_resp)
    resp_spec = jnp.dot(resp.reshape(-1, angles), forward, precision=HIGH).reshape(frame_count, tilt_count, 2 * angles)
    responsibility_real, responsibility_imaginary = (resp_spec[..., :angles], resp_spec[..., angles:])
    back_projection = spectral_cross_terms(frame_real, frame_imaginary, responsibility_real, responsibility_imaginary, 'sha,sxa->xha')
    numer = jnp.dot(back_projection.reshape(-1, 2 * angles), inverse, precision=HIGH).reshape(tilt_count, shells, angles)
    weight = lax.optimization_barrier(jnp.sum(resp, axis=(0, 2)))
    new_slices = (numer + slices) / (weight[:, None, None] + 1.0)
    return (log_resp, new_slices)
```

```python
import functools
import math

import jax
import jax.numpy as jnp
import numpy as np
from jax import lax
from jax.experimental import pallas as pl
from jax.experimental.pallas import tpu as pltpu
from jax.sharding import PartitionSpec as P

F32, BF16 = jnp.float32, jnp.bfloat16
MESH = pl.DeviceIdType.MESH
LANES = 128


def packed_tables(angles):
    half, quarter = angles // 2, angles // 4
    p, g = np.arange(half)[:, None], np.arange(quarter)[None, :]
    even_phase = 2.0 * np.pi * ((p * g) % half) / half
    even = np.concatenate([np.cos(even_phase), -np.sin(even_phase)], axis=1)
    even[:, quarter] = 1.0 - 2.0 * (np.arange(half) % 2)
    odd_phase = 2.0 * np.pi * ((p * (2 * g + 1)) % angles) / angles
    odd = np.concatenate([np.cos(odd_phase), -np.sin(odd_phase)], axis=1)
    parts = []
    for table in (even, odd):
        high = table.astype(BF16)
        parts += [high, (table - high.astype(np.float64)).astype(BF16)]
    forward = np.stack(parts)
    return forward, np.ascontiguousarray(forward.transpose(0, 2, 1))


def mm(a, b):
    return jnp.dot(a, b, preferred_element_type=F32)


def split(x):
    high = x.astype(BF16)
    return high, (x - high.astype(F32)).astype(BF16)


def mm3(x, high, low):
    xh, xl = split(x)
    return mm(xh, high) + mm(xl, high) + mm(xh, low)


def lse_of(rows):
    top = functools.reduce(jnp.maximum, rows)
    return top + jnp.log(functools.reduce(jnp.add, [jnp.exp(r - top) for r in rows]))


def kernel(
    nx, frames, slices, ftab_hbm, itab_hbm, logp, new,
    fr, sl, ft, it, X, Y, acc, pb, sc, lsx, lsz, sa, ra, sb, rb,
    fsem, msem, xs, xr, zs, zr, as_, ar, bs, br,
):
    K, R, N = fr.shape
    T, H = sl.shape[0], N // 2
    dp, rot = lax.axis_index("dp"), lax.axis_index("rot")
    ny, nz = lax.axis_size("dp") // 2, lax.axis_size("rot") // nx
    y, core = dp // 2, dp % 2
    z, x = rot // nx, rot % nx
    share = R // (2 * ny)
    chunks = share // 8
    body = T * 4 * chunks

    c_ft = pltpu.make_async_copy(ftab_hbm, ft, msem.at[0])
    c_sl = pltpu.make_async_copy(slices, sl, msem.at[1])
    c_it = pltpu.make_async_copy(itab_hbm, it, msem.at[2])
    c_sl.start()
    c_ft.start()
    for k in range(K):
        pltpu.make_async_copy(frames.at[k], fr.at[k], fsem.at[k]).start()
    c_it.start()

    barrier = pltpu.get_barrier_semaphore()
    peers = [(dp, z * nx + (x + d) % nx) for d in range(1, nx)]
    peers += [(dp, ((z + d) % nz) * nx + x) for d in range(1, nz)]
    peers += [(y * 2 + 1 - core, rot)]
    peers += [(((y + d) % ny) * 2 + core, rot) for d in range(1, ny)]
    for peer in peers:
        pl.semaphore_signal(barrier, inc=1, device_id=peer, device_id_type=MESH)

    c_sl.wait()
    c_ft.wait()
    lane = lax.broadcasted_iota(jnp.int32, (R, LANES), 1)
    totals = []
    for t in range(T):
        values = sl[t]
        totals.append(jnp.sum(jnp.sum(values, axis=0, keepdims=True), axis=1, keepdims=True))
        logs = jnp.log(values)
        even, odd = logs[:, :H] + logs[:, H:], logs[:, :H] - logs[:, H:]
        eh, em = split(even)
        el = (even - eh.astype(F32) - em.astype(F32)).astype(BF16)
        ye = mm(eh, ft[0]) + mm(em, ft[0]) + mm(el, ft[0]) + mm(eh, ft[1])
        yo = mm3(odd, ft[2], ft[3])
        re, im = ye[:, :LANES], ye[:, LANES:]
        Y[t, 0] = re
        Y[t, 1] = jnp.where(lane == 0, 0.0, im)
        Y[t, 2] = jnp.where(lane == 0, im, re)
        Y[t, 3] = yo[:, :LANES]
        Y[t, 4] = yo[:, LANES:]

    @pl.loop(0, K)
    def _(k):
        pltpu.make_async_copy(frames.at[k], fr.at[k], fsem.at[k]).wait()
        left, right = fr[k, :, :H], fr[k, :, H:]
        xe = mm((left + right).astype(F32).astype(BF16), ft[0])
        xo = mm((left - right).astype(F32).astype(BF16), ft[2])
        X[k, 0] = xe[:, :LANES]
        X[k, 1] = xe[:, LANES:]
        X[k, 2] = xo[:, :LANES]
        X[k, 3] = xo[:, LANES:]
        sums = [None] * (4 * T)
        for c in range(R // 8):
            rows = slice(8 * c, 8 * c + 8)
            er, ei, o_r, oi = (X[k, j, rows] for j in range(4))
            for t in range(T):
                yr, yb, yc, zr_, zi = (Y[t, j, rows] for j in range(5))
                terms = (er * yr + ei * yb, ei * yc - er * yb, o_r * zr_ + oi * zi, oi * zr_ - o_r * zi)
                for j in range(4):
                    n = 4 * t + j
                    sums[n] = terms[j] if c == 0 else sums[n] + terms[j]
        for t in range(T):
            for j in range(4):
                acc[j, pl.ds(pl.multiple_of((t * K + k) * 8, 8), 8)] = sums[4 * t + j]

    rows = T * K
    lane = lax.broadcasted_iota(jnp.int32, (rows, LANES), 1)

    def gathered(j):
        return functools.reduce(
            jnp.add, [acc[j, pl.ds(s, rows, stride=8)] for s in range(8)]
        )

    cer, cei, cor, coi = (gathered(j) for j in range(4))
    total = jnp.concatenate([jnp.broadcast_to(v, (K, 1)) for v in totals], axis=0)
    base = cer[:, :1] * (1.0 / N) - total
    scale, edge = 2.0 / N, 1.0 / N
    ce = jnp.concatenate(
        [jnp.where(lane == 0, 0.0, cer * scale), cei * jnp.where(lane == 0, edge, scale)], axis=1
    )
    co = jnp.concatenate([cor * scale, coi * scale], axis=1)
    c_it.wait()
    u = mm3(ce, it[0], it[1])
    v = mm3(co, it[2], it[3])
    anneal = 4.0 / math.sqrt(R * N)
    low, high = anneal * (base + (u + v)), anneal * (base + (u - v))
    sc[:, :H] = low
    sc[:, H:] = high
    top = jnp.max(jnp.maximum(low, high), axis=1, keepdims=True)
    top = functools.reduce(jnp.maximum, [top[t * K : t * K + K] for t in range(T)])
    top_rows = jnp.concatenate([top] * T, axis=0)
    low, high = jnp.exp(low - top_rows), jnp.exp(high - top_rows)
    mass = jnp.sum(low + high, axis=1, keepdims=True)
    local = top + jnp.log(functools.reduce(jnp.add, [mass[t * K : t * K + K] for t in range(T)]))
    diagonal = lax.broadcasted_iota(jnp.int32, (K, LANES), 0) == lax.broadcasted_iota(
        jnp.int32, (K, LANES), 1
    )
    lsx[x] = jnp.sum(jnp.where(diagonal, local, 0.0), axis=0, keepdims=True)

    pl.semaphore_wait(barrier, len(peers))
    x_copies = []
    for d in range(1, nx):
        x_copies.append(
            pltpu.make_async_remote_copy(
                lsx.at[x], lsx.at[x], xs.at[d - 1], xr.at[d - 1],
                device_id=(dp, z * nx + (x + d) % nx), device_id_type=MESH,
            )
        )
        x_copies[-1].start()

    pe = mm3(low + high, ft[0], ft[1])
    po = mm3(low - high, ft[2], ft[3])

    for copy in x_copies:
        copy.wait_recv()
    lsz[z] = lse_of([lsx[i] for i in range(nx)])
    z_copies = []
    for d in sorted(range(1, nz), key=lambda d: -min(d, nz - d)):
        z_copies.append(
            pltpu.make_async_remote_copy(
                lsz.at[z], lsz.at[z], zs.at[d - 1], zr.at[d - 1],
                device_id=(dp, ((z + d) % nz) * nx + x), device_id_type=MESH,
            )
        )
        z_copies[-1].start()
    for copy in z_copies:
        copy.wait_recv()
    lse_row = lse_of([lsz[i] for i in range(nz)])
    lse = jnp.sum(jnp.where(diagonal, lse_row, 0.0), axis=1, keepdims=True)
    factor = jnp.exp(top - lse)
    factor_rows = jnp.concatenate([factor] * T, axis=0)
    pe, po = pe * factor_rows, po * factor_rows
    re, im = pe[:, :LANES], pe[:, LANES:]
    spectra = (
        re,
        jnp.where(lane == 0, 0.0, im),
        jnp.where(lane == 0, im, re),
        po[:, :LANES],
        po[:, LANES:],
    )
    for t in range(T):
        for j in range(5):
            for k in range(K):
                n = t * K + k
                pb[t, j, k] = jnp.broadcast_to(spectra[j][n : n + 1], (8, LANES))
    mass = mass * factor_rows
    weights = [jnp.sum(mass[t * K : t * K + K], axis=0, keepdims=True) for t in range(T)]
    weight_tile = jnp.concatenate(
        [jnp.broadcast_to(w, (8 // T, LANES)) for w in weights], axis=0
    )

    def back(owner):
        tiles = [None] * body
        for k in range(K):
            ps = [[pb[t, j, k] for j in range(5)] for t in range(T)]
            for c in range(chunks):
                rows = pl.ds(pl.multiple_of(owner * share + 8 * c, 8), 8)
                er, ei, o_r, oi = (X[k, j, rows] for j in range(4))
                for t in range(T):
                    pr, pb_, pc, qr, qi = ps[t]
                    terms = (er * pr + ei * pb_, ei * pc - er * pb_, o_r * qr + oi * qi, oi * qr - o_r * qi)
                    for j in range(4):
                        n = (t * 4 + j) * chunks + c
                        tiles[n] = terms[j] if k == 0 else tiles[n] + terms[j]
        return tiles

    order = sorted(range(1, ny), key=lambda d: -min(d, ny - d)) + [0]

    def to_core(d):
        return pltpu.make_async_remote_copy(
            sa.at[d], ra.at[d], as_.at[d], ar.at[d],
            device_id=(y * 2 + 1 - core, rot), device_id_type=MESH,
        )

    def to_chip(d):
        return pltpu.make_async_remote_copy(
            sb.at[d - 1], rb.at[d - 1], bs.at[d - 1], br.at[d - 1],
            device_id=(((y + d) % ny) * 2 + core, rot), device_id_type=MESH,
        )

    for d in order:
        for n, tile in enumerate(back(((y + d) % ny) * 2 + 1 - core)):
            sa[d, n] = tile
        sa[d, body] = weight_tile
        to_core(d).start()
    for d in order:
        tiles = back(((y + d) % ny) * 2 + core) + [weight_tile]
        to_core(d).wait_recv()
        tiles = [tile + ra[d, n] for n, tile in enumerate(tiles)]
        if d:
            for n, tile in enumerate(tiles):
                sb[d - 1, n] = tile
            to_chip(d).start()

    scores = sc[...] - jnp.concatenate([lse] * T, axis=0)
    for t in range(T):
        for q in range(N // LANES):
            logp[pl.ds(q * T + t, K, stride=T * N // LANES)] = scores[
                t * K : t * K + K, q * LANES : (q + 1) * LANES
            ]

    for d in order[:-1]:
        to_chip(d).wait_recv()
        tiles = [tile + rb[d - 1, n] for n, tile in enumerate(tiles)]
    parts = []
    for j in range(4):
        parts.append(
            jnp.concatenate(
                [tiles[(t * 4 + j) * chunks + c] for t in range(T) for c in range(chunks)], axis=0
            )
        )
    lane = lax.broadcasted_iota(jnp.int32, parts[0].shape, 1)
    ends = jnp.where(lane == 0, edge, scale)
    u = mm3(jnp.concatenate([parts[0] * ends, parts[1] * ends], axis=1), it[0], it[1])
    v = mm3(jnp.concatenate([parts[2] * scale, parts[3] * scale], axis=1), it[2], it[3])
    mine = pl.ds(pl.multiple_of(dp * share, 8), share)
    for t in range(T):
        rows = slice(t * share, (t + 1) * share)
        weight = tiles[body][t * (8 // T) : t * (8 // T) + 1, :1] + 1.0
        new[t, :, :H] = (u[rows] + v[rows] + sl[t, mine, :H]) / weight
        new[t, :, H:] = (u[rows] - v[rows] + sl[t, mine, H:]) / weight

    for copy in x_copies + z_copies:
        copy.wait_send()
    for d in order:
        to_core(d).wait_send()
    for d in order[:-1]:
        to_chip(d).wait_send()


def on_device(nx, frames, slices):
    K, R, N = frames.shape
    T = slices.shape[0]
    ny, nz = lax.axis_size("dp") // 2, lax.axis_size("rot") // nx
    share = R // (2 * ny)
    body = T * 4 * (share // 8)
    forward, inverse = packed_tables(N)
    anywhere = pl.BlockSpec(memory_space=pl.ANY)
    vmem = pl.BlockSpec(memory_space=pltpu.VMEM)
    dma = pltpu.SemaphoreType.DMA
    hops = max(nz - 1, 1)
    steps = max(ny - 1, 1)
    logp, new = pl.pallas_call(
        functools.partial(kernel, nx),
        out_shape=(
            jax.ShapeDtypeStruct((K * T * N // LANES, LANES), F32),
            jax.ShapeDtypeStruct((T, share, N), F32),
        ),
        in_specs=[anywhere] * 4,
        out_specs=(vmem, vmem),
        scratch_shapes=[
            pltpu.VMEM((K, R, N), jnp.int32),
            pltpu.VMEM((T, R, N), F32),
            pltpu.VMEM((4, N // 2, N // 2), BF16),
            pltpu.VMEM((4, N // 2, N // 2), BF16),
            pltpu.VMEM((K, 4, R, LANES), F32),
            pltpu.VMEM((T, 5, R, LANES), F32),
            pltpu.VMEM((4, T * K * 8, LANES), F32),
            pltpu.VMEM((T, 5, K, 8, LANES), F32),
            pltpu.VMEM((T * K, N), F32),
            pltpu.VMEM((nx, 1, LANES), F32),
            pltpu.VMEM((nz, 1, LANES), F32),
            pltpu.VMEM((ny, body + 1, 8, LANES), F32),
            pltpu.VMEM((ny, body + 1, 8, LANES), F32),
            pltpu.VMEM((steps, body + 1, 8, LANES), F32),
            pltpu.VMEM((steps, body + 1, 8, LANES), F32),
            dma((K,)),
            dma((3,)),
            dma((nx - 1,)),
            dma((nx - 1,)),
            dma((hops,)),
            dma((hops,)),
            dma((ny,)),
            dma((ny,)),
            dma((steps,)),
            dma((steps,)),
        ],
        compiler_params=pltpu.CompilerParams(
            collective_id=0, has_side_effects=True, vmem_limit_bytes=67_043_328
        ),
    )(frames, slices, forward, inverse)
    log_resp = logp.reshape(K, N // LANES, T, LANES).transpose(0, 2, 1, 3).reshape(K, T, N)
    return log_resp, new


def solution(mesh, nx=4):
    in_specs = (P("dp", None, None), P("rot", None, None))
    out_specs = (P("dp", "rot", None), P("rot", "dp", None))
    return jax.shard_map(
        functools.partial(on_device, nx),
        mesh=mesh, in_specs=in_specs, out_specs=out_specs, check_vma=False,
    )
```

```python
import functools
import math

import jax
import jax.numpy as jnp
import numpy as np
from jax import lax
from jax.experimental import pallas as pl
from jax.experimental.pallas import tpu as pltpu
from jax.sharding import PartitionSpec as P

F32, BF16 = jnp.float32, jnp.bfloat16
MESH = pl.DeviceIdType.MESH
LANES = 128
GROUP = 4


def packed_tables(angles):
    half, quarter = angles // 2, angles // 4
    p, g = np.arange(half)[:, None], np.arange(quarter)[None, :]
    even_phase = 2.0 * np.pi * ((p * g) % half) / half
    even = np.concatenate([np.cos(even_phase), -np.sin(even_phase)], axis=1)
    even[:, quarter] = 1.0 - 2.0 * (np.arange(half) % 2)
    odd_phase = 2.0 * np.pi * ((p * (2 * g + 1)) % angles) / angles
    odd = np.concatenate([np.cos(odd_phase), -np.sin(odd_phase)], axis=1)
    parts = []
    for table in (even, odd):
        high = table.astype(BF16)
        parts += [high, (table - high.astype(np.float64)).astype(BF16)]
    forward = np.stack(parts)
    return forward, np.ascontiguousarray(forward.transpose(0, 2, 1))


def mm(a, b):
    return jnp.dot(a, b, preferred_element_type=F32)


def split(x):
    high = x.astype(BF16)
    return high, (x - high.astype(F32)).astype(BF16)


def mm3(x, high, low):
    xh, xl = split(x)
    return mm(xh, high) + mm(xl, high) + mm(xh, low)


def three(re, im, first):
    if first is None:
        return re, re + im, re - im
    return re, jnp.where(first, re, re + im), jnp.where(first, im, re - im)


def joined(sums, first):
    one, two, last = sums
    re, im = one - last, one - two
    if first is None:
        return re, im
    return jnp.where(first, two, re), jnp.where(first, last, im)


def lse_of(rows):
    top = functools.reduce(jnp.maximum, rows)
    return top + jnp.log(functools.reduce(jnp.add, [jnp.exp(r - top) for r in rows]))


def kernel(
    nx, frames, slices, ftab_hbm, itab_hbm, logp, new,
    fr, sl, ft, it, X, Y, acc, pb, sc, lsx, lsz, sa, ra, sb, rb,
    fsem, msem, xs, xr, zs, zr, as_, ar, bs, br,
):
    K, R, N = fr.shape
    T, H = sl.shape[0], N // 2
    dp, rot = lax.axis_index("dp"), lax.axis_index("rot")
    ny, nz = lax.axis_size("dp") // 2, lax.axis_size("rot") // nx
    y, core = dp // 2, dp % 2
    z, x = rot // nx, rot % nx
    share = R // (2 * ny)
    chunks = share // 8
    body = T * 4 * chunks

    c_ft = pltpu.make_async_copy(ftab_hbm, ft, msem.at[0])
    c_sl = pltpu.make_async_copy(slices, sl, msem.at[1])
    c_it = pltpu.make_async_copy(itab_hbm, it, msem.at[2])
    c_sl.start()
    c_ft.start()

    def group_copy(g):
        part = pl.ds(g * GROUP, GROUP)
        return pltpu.make_async_copy(frames.at[part], fr.at[part], fsem.at[g])

    @pl.loop(0, K // GROUP)
    def _(g):
        group_copy(g).start()

    barrier = pltpu.get_barrier_semaphore()
    peers = [(dp, z * nx + (x + d) % nx) for d in range(1, nx)]
    peers += [(dp, ((z + d) % nz) * nx + x) for d in range(1, nz)]
    peers += [(y * 2 + 1 - core, rot)]
    peers += [(((y + d) % ny) * 2 + core, rot) for d in range(1, ny)]
    for peer in peers:
        pl.semaphore_signal(barrier, inc=1, device_id=peer, device_id_type=MESH)

    c_sl.wait()
    c_ft.wait()
    c_it.start()
    first = lax.broadcasted_iota(jnp.int32, (R, LANES), 1) == 0
    totals = []
    for t in range(T):
        values = sl[t]
        totals.append(jnp.sum(jnp.sum(values, axis=0, keepdims=True), axis=1, keepdims=True))
        logs = jnp.log(values)
        even, odd = logs[:, :H] + logs[:, H:], logs[:, :H] - logs[:, H:]
        eh, em = split(even)
        el = (even - eh.astype(F32) - em.astype(F32)).astype(BF16)
        ye = mm(eh, ft[0]) + mm(em, ft[0]) + mm(el, ft[0]) + mm(eh, ft[1])
        yo = mm3(odd, ft[2], ft[3])
        pairs = three(ye[:, :LANES], ye[:, LANES:], first)
        pairs += three(yo[:, :LANES], yo[:, LANES:], None)
        for j in range(6):
            Y[t, j] = pairs[j]

    @pl.loop(0, K // GROUP)
    def _(g):
        group_copy(g).wait()
        part = pl.ds(g * GROUP, GROUP)
        left = fr[part, :, :H].astype(F32).astype(BF16).reshape(GROUP * R, H)
        right = fr[part, :, H:].astype(F32).astype(BF16).reshape(GROUP * R, H)
        outs = mm(left + right, ft[0]), mm(left - right, ft[2])
        for i in range(GROUP):
            k = g * GROUP + i
            sums = [None] * (6 * T)
            for c in range(R // 8):
                rows = slice(8 * c, 8 * c + 8)
                for half, out in enumerate(outs):
                    tile = out[i * R + 8 * c : i * R + 8 * c + 8]
                    re, im = tile[:, :LANES], tile[:, LANES:]
                    for j, value in zip(range(3 * half, 3 * half + 3), (re + im, re, im)):
                        X[k, j, rows] = value
                        for t in range(T):
                            n, term = t * 6 + j, value * Y[t, j, rows]
                            sums[n] = term if c == 0 else sums[n] + term
            for t in range(T):
                for j in range(6):
                    acc[j, pl.ds(pl.multiple_of((t * K + k) * 8, 8), 8)] = sums[t * 6 + j]

    rows = T * K
    lane = lax.broadcasted_iota(jnp.int32, (rows, LANES), 1)

    def gathered(j):
        return functools.reduce(
            jnp.add, [acc[j, pl.ds(s, rows, stride=8)] for s in range(8)]
        )

    gathers = [gathered(j) for j in range(6)]
    cer, cei = joined(gathers[:3], lane == 0)
    cor, coi = joined(gathers[3:], None)
    total = jnp.concatenate([jnp.broadcast_to(v, (K, 1)) for v in totals], axis=0)
    base = cer[:, :1] * (1.0 / N) - total
    scale, edge = 2.0 / N, 1.0 / N
    ce = jnp.concatenate(
        [jnp.where(lane == 0, 0.0, cer * scale), cei * jnp.where(lane == 0, edge, scale)], axis=1
    )
    co = jnp.concatenate([cor * scale, coi * scale], axis=1)
    c_it.wait()
    u = mm3(ce, it[0], it[1])
    v = mm3(co, it[2], it[3])
    anneal = 4.0 / math.sqrt(R * N)
    low, high = anneal * (base + (u + v)), anneal * (base + (u - v))
    sc[:, :H] = low
    sc[:, H:] = high
    top = jnp.max(jnp.maximum(low, high), axis=1, keepdims=True)
    top = functools.reduce(jnp.maximum, [top[t * K : t * K + K] for t in range(T)])
    top_rows = jnp.concatenate([top] * T, axis=0)
    low, high = jnp.exp(low - top_rows), jnp.exp(high - top_rows)
    mass = jnp.sum(low + high, axis=1, keepdims=True)
    local = top + jnp.log(functools.reduce(jnp.add, [mass[t * K : t * K + K] for t in range(T)]))
    diagonal = lax.broadcasted_iota(jnp.int32, (K, LANES), 0) == lax.broadcasted_iota(
        jnp.int32, (K, LANES), 1
    )
    lsx[x] = jnp.sum(jnp.where(diagonal, local, 0.0), axis=0, keepdims=True)

    pl.semaphore_wait(barrier, len(peers))
    x_copies = []
    for d in range(1, nx):
        x_copies.append(
            pltpu.make_async_remote_copy(
                lsx.at[x], lsx.at[x], xs.at[d - 1], xr.at[d - 1],
                device_id=(dp, z * nx + (x + d) % nx), device_id_type=MESH,
            )
        )
        x_copies[-1].start()

    pe = mm3(low + high, ft[0], ft[1])
    po = mm3(low - high, ft[2], ft[3])

    for copy in x_copies:
        copy.wait_recv()
    lsz[z] = lse_of([lsx[i] for i in range(nx)])
    z_copies = []
    for d in sorted(range(1, nz), key=lambda d: -min(d, nz - d)):
        z_copies.append(
            pltpu.make_async_remote_copy(
                lsz.at[z], lsz.at[z], zs.at[d - 1], zr.at[d - 1],
                device_id=(dp, ((z + d) % nz) * nx + x), device_id_type=MESH,
            )
        )
        z_copies[-1].start()
    for copy in z_copies:
        copy.wait_recv()
    lse_row = lse_of([lsz[i] for i in range(nz)])
    lse = jnp.sum(jnp.where(diagonal, lse_row, 0.0), axis=1, keepdims=True)
    factor = jnp.exp(top - lse)
    factor_rows = jnp.concatenate([factor] * T, axis=0)
    pe, po = pe * factor_rows, po * factor_rows
    spectra = three(pe[:, :LANES], pe[:, LANES:], lane == 0)
    spectra += three(po[:, :LANES], po[:, LANES:], None)
    for j in range(6):
        pb[j] = spectra[j]
    mass = mass * factor_rows
    weights = [jnp.sum(mass[t * K : t * K + K], axis=0, keepdims=True) for t in range(T)]
    weight_tile = jnp.concatenate(
        [jnp.broadcast_to(w, (8 // T, LANES)) for w in weights], axis=0
    )

    first = lax.broadcasted_iota(jnp.int32, (8, LANES), 1) == 0

    def back(owner):
        sums = [[[None] * 6 for c in range(chunks)] for t in range(T)]
        for k in range(K):
            ps = [[pb[j, pl.ds(t * K + k, 8, stride=0)] for j in range(6)] for t in range(T)]
            for c in range(chunks):
                rows = pl.ds(pl.multiple_of(owner * share + 8 * c, 8), 8)
                for j in range(6):
                    x_ = X[k, j, rows]
                    for t in range(T):
                        term = x_ * ps[t][j]
                        sums[t][c][j] = term if k == 0 else sums[t][c][j] + term
        tiles = [None] * body
        for t in range(T):
            for c in range(chunks):
                parts = joined(sums[t][c][:3], first) + joined(sums[t][c][3:], None)
                for j in range(4):
                    tiles[(t * 4 + j) * chunks + c] = parts[j]
        return tiles

    order = sorted(range(1, ny), key=lambda d: -min(d, ny - d)) + [0]

    def to_core(d):
        return pltpu.make_async_remote_copy(
            sa.at[d], ra.at[d], as_.at[d], ar.at[d],
            device_id=(y * 2 + 1 - core, rot), device_id_type=MESH,
        )

    def to_chip(d):
        return pltpu.make_async_remote_copy(
            sb.at[d - 1], rb.at[d - 1], bs.at[d - 1], br.at[d - 1],
            device_id=(((y + d) % ny) * 2 + core, rot), device_id_type=MESH,
        )

    for d in order:
        for n, tile in enumerate(back(((y + d) % ny) * 2 + 1 - core)):
            sa[d, n] = tile
        sa[d, body] = weight_tile
        to_core(d).start()
    for d in order:
        tiles = back(((y + d) % ny) * 2 + core) + [weight_tile]
        to_core(d).wait_recv()
        tiles = [tile + ra[d, n] for n, tile in enumerate(tiles)]
        if d:
            for n, tile in enumerate(tiles):
                sb[d - 1, n] = tile
            to_chip(d).start()

    scores = sc[...] - jnp.concatenate([lse] * T, axis=0)
    for t in range(T):
        for q in range(N // LANES):
            logp[pl.ds(q * T + t, K, stride=T * N // LANES)] = scores[
                t * K : t * K + K, q * LANES : (q + 1) * LANES
            ]

    for d in order[:-1]:
        to_chip(d).wait_recv()
        tiles = [tile + rb[d - 1, n] for n, tile in enumerate(tiles)]
    parts = []
    for j in range(4):
        parts.append(
            jnp.concatenate(
                [tiles[(t * 4 + j) * chunks + c] for t in range(T) for c in range(chunks)], axis=0
            )
        )
    lane = lax.broadcasted_iota(jnp.int32, parts[0].shape, 1)
    ends = jnp.where(lane == 0, edge, scale)
    u = mm3(jnp.concatenate([parts[0] * ends, parts[1] * ends], axis=1), it[0], it[1])
    v = mm3(jnp.concatenate([parts[2] * scale, parts[3] * scale], axis=1), it[2], it[3])
    mine = pl.ds(pl.multiple_of(dp * share, 8), share)
    for t in range(T):
        rows = slice(t * share, (t + 1) * share)
        weight = tiles[body][t * (8 // T) : t * (8 // T) + 1, :1] + 1.0
        new[t, :, :H] = (u[rows] + v[rows] + sl[t, mine, :H]) / weight
        new[t, :, H:] = (u[rows] - v[rows] + sl[t, mine, H:]) / weight

    for copy in x_copies + z_copies:
        copy.wait_send()
    for d in order:
        to_core(d).wait_send()
    for d in order[:-1]:
        to_chip(d).wait_send()


def hand_over(logp, new, logp_out, new_out, sem):
    copies = [
        pltpu.make_async_copy(logp, logp_out, sem.at[0]),
        pltpu.make_async_copy(new, new_out, sem.at[1]),
    ]
    for copy in copies:
        copy.start()
    for copy in copies:
        copy.wait()


def on_device(nx, frames, slices):
    K, R, N = frames.shape
    T = slices.shape[0]
    ny, nz = lax.axis_size("dp") // 2, lax.axis_size("rot") // nx
    share = R // (2 * ny)
    body = T * 4 * (share // 8)
    forward, inverse = packed_tables(N)
    hbm = pl.BlockSpec(memory_space=pltpu.HBM)
    vmem = pl.BlockSpec(memory_space=pltpu.VMEM)
    dma = pltpu.SemaphoreType.DMA
    hops = max(nz - 1, 1)
    steps = max(ny - 1, 1)
    logp, new = pl.pallas_call(
        functools.partial(kernel, nx),
        out_shape=(
            jax.ShapeDtypeStruct((K * T * N // LANES, LANES), F32),
            jax.ShapeDtypeStruct((T, share, N), F32),
        ),
        in_specs=[hbm] * 4,
        out_specs=(vmem, vmem),
        scratch_shapes=[
            pltpu.VMEM((K, R, N), jnp.int32),
            pltpu.VMEM((T, R, N), F32),
            pltpu.VMEM((4, N // 2, N // 2), BF16),
            pltpu.VMEM((4, N // 2, N // 2), BF16),
            pltpu.VMEM((K, 6, R, LANES), F32),
            pltpu.VMEM((T, 6, R, LANES), F32),
            pltpu.VMEM((6, 8 * T * K, LANES), F32),
            pltpu.VMEM((6, T * K, LANES), F32),
            pltpu.VMEM((T * K, N), F32),
            pltpu.VMEM((nx, 1, LANES), F32),
            pltpu.VMEM((nz, 1, LANES), F32),
            pltpu.VMEM((ny, body + 1, 8, LANES), F32),
            pltpu.VMEM((ny, body + 1, 8, LANES), F32),
            pltpu.VMEM((steps, body + 1, 8, LANES), F32),
            pltpu.VMEM((steps, body + 1, 8, LANES), F32),
            dma((K // GROUP,)),
            dma((3,)),
            dma((nx - 1,)),
            dma((nx - 1,)),
            dma((hops,)),
            dma((hops,)),
            dma((ny,)),
            dma((ny,)),
            dma((steps,)),
            dma((steps,)),
        ],
        compiler_params=pltpu.CompilerParams(
            collective_id=0, has_side_effects=True, vmem_limit_bytes=32 << 20
        ),
    )(*(pltpu.with_memory_space_constraint(v, pltpu.HBM) for v in (frames, slices, jnp.asarray(forward), jnp.asarray(inverse))))
    logp, new = pl.pallas_call(
        hand_over,
        out_shape=(
            jax.ShapeDtypeStruct(logp.shape, F32),
            jax.ShapeDtypeStruct(new.shape, F32),
        ),
        in_specs=[vmem, vmem],
        out_specs=(hbm, hbm),
        scratch_shapes=[dma((2,))],
        compiler_params=pltpu.CompilerParams(vmem_limit_bytes=1 << 20),
    )(logp, new)
    log_resp = logp.reshape(K, N // LANES, T, LANES).transpose(0, 2, 1, 3).reshape(K, T, N)
    return log_resp, new


def solution(mesh, nx=4):
    in_specs = (P("dp", None, None), P("rot", None, None))
    out_specs = (P("dp", "rot", None), P("rot", "dp", None))
    return jax.shard_map(
        functools.partial(on_device, nx),
        mesh=mesh, in_specs=in_specs, out_specs=out_specs, check_vma=False,
    )
```

```python
import functools
import math

import jax
import jax.numpy as jnp
import numpy as np
from jax import lax
from jax.experimental import pallas as pl
from jax.experimental.pallas import tpu as pltpu
from jax.sharding import PartitionSpec as P

F32, BF16 = jnp.float32, jnp.bfloat16
MESH = pl.DeviceIdType.MESH
LANES = 128
GROUP = 4


def packed_tables(angles):
    half, quarter = angles // 2, angles // 4
    p, g = np.arange(half)[:, None], np.arange(quarter)[None, :]
    even_phase = 2.0 * np.pi * ((p * g) % half) / half
    even = np.concatenate([np.cos(even_phase), -np.sin(even_phase)], axis=1)
    even[:, quarter] = 1.0 - 2.0 * (np.arange(half) % 2)
    odd_phase = 2.0 * np.pi * ((p * (2 * g + 1)) % angles) / angles
    odd = np.concatenate([np.cos(odd_phase), -np.sin(odd_phase)], axis=1)
    parts = []
    for table in (even, odd):
        high = table.astype(BF16)
        parts += [high, (table - high.astype(np.float64)).astype(BF16)]
    forward = np.stack(parts)
    return forward, np.ascontiguousarray(forward.transpose(0, 2, 1))


def mm(a, b):
    return jnp.dot(a, b, preferred_element_type=F32)


def split(x):
    high = x.astype(BF16)
    return high, (x - high.astype(F32)).astype(BF16)


def mm3(x, high, low):
    return mm_parts(split(x), high, low)


def mm_parts(parts, high, low):
    rows = parts[0].shape[0]
    stacked = mm(jnp.concatenate(parts, axis=0), high)
    total = mm(parts[0], low)
    for i in reversed(range(len(parts))):
        total = total + stacked[i * rows : (i + 1) * rows]
    return total


def three(re, im, first):
    if first is None:
        return re, re + im, re - im
    return re, jnp.where(first, re, re + im), jnp.where(first, im, re - im)


def joined(sums, first):
    one, two, last = sums
    re, im = one - last, one - two
    if first is None:
        return re, im
    return jnp.where(first, two, re), jnp.where(first, last, im)


def kernel(
    nx, frames, slices, ftab_hbm, itab_hbm, logp, new,
    fr, sl, ft, it, X, Y, acc, pb, sc, ls, fin, wt, sa, ra, sb, rb,
    fsem, msem, ls_sem, fin_sem, wt_sem, as_, ar, bs, br,
):
    K, R, N = fr.shape
    T, H = sl.shape[0], N // 2
    dp, rot = lax.axis_index("dp"), lax.axis_index("rot")
    ny, nz = lax.axis_size("dp") // 2, lax.axis_size("rot") // nx
    y, core = dp // 2, dp % 2
    z, x = rot // nx, rot % nx
    share = R // (2 * ny)
    chunks, half = share // 8, T * 4
    body = half * chunks

    c_ft = pltpu.make_async_copy(ftab_hbm, ft, msem.at[0])
    c_sl = pltpu.make_async_copy(slices, sl, msem.at[1])
    c_it = pltpu.make_async_copy(itab_hbm, it, msem.at[2])
    for i in range(4):
        for t in range(T):
            part = pl.ds(i * R // 4, R // 4)
            pltpu.make_async_copy(slices.at[t, part], sl.at[t, part], msem.at[1]).start()
        pltpu.make_async_copy(ftab_hbm.at[i], ft.at[i], msem.at[0]).start()

    def group_copy(g):
        part = pl.ds(g * GROUP, GROUP)
        return pltpu.make_async_copy(frames.at[part], fr.at[part], fsem.at[g])

    barrier = pltpu.get_barrier_semaphore()
    low_z = nz // 2
    lower = z < low_z
    steps = [(i, j) for i in range(low_z) for j in range(nx)]
    steps.sort(key=lambda s: -(min(s[0], low_z - s[0]) + min(s[1], nx - s[1])))

    def at(i, j, upper=0):
        return dp, ((z + i) % low_z + upper * low_z) * nx + (x + j) % nx

    mine = [at(i, j) for i, j in steps if i or j]
    opposite = [at(i, j, 1) for i, j in steps]
    family = [((dp + d) % (2 * ny), rot) for d in range(1, 2 * ny)]
    def signal(peer):
        pl.semaphore_signal(barrier, inc=1, device_id=peer, device_id_type=MESH)

    @pl.when(lower)
    def _():
        for peer in opposite + mine:
            signal(peer)

    for peer in family:
        signal(peer)

    @pl.loop(0, K)
    def _(k):
        pltpu.make_async_copy(frames.at[k], fr.at[k], fsem.at[k // GROUP]).start()

    c_it.start()

    c_sl.wait()
    c_ft.wait()
    first = lax.broadcasted_iota(jnp.int32, (R, LANES), 1) == 0
    totals = []
    for t in range(T):
        values = sl[t]
        totals.append(jnp.sum(jnp.sum(values, axis=0, keepdims=True), axis=1, keepdims=True))
        logs = jnp.log(values)
        even, odd = logs[:, :H] + logs[:, H:], logs[:, :H] - logs[:, H:]
        eh, em = split(even)
        el = (even - eh.astype(F32) - em.astype(F32)).astype(BF16)
        ye = mm_parts((eh, em, el), ft[0], ft[1])
        yo = mm3(odd, ft[2], ft[3])
        pairs = three(ye[:, :LANES], ye[:, LANES:], first)
        pairs += three(yo[:, :LANES], yo[:, LANES:], None)
        for j in range(6):
            Y[t, j] = pairs[j]

    @pl.loop(0, K // GROUP)
    def _(g):
        group_copy(g).wait()
        part = pl.ds(g * GROUP, GROUP)
        left = fr[part, :, :H].astype(F32).astype(BF16).reshape(GROUP * R, H)
        right = fr[part, :, H:].astype(F32).astype(BF16).reshape(GROUP * R, H)
        outs = mm(left + right, ft[0]), mm(left - right, ft[2])
        for i in range(GROUP):
            k = g * GROUP + i
            sums = [None] * (6 * T)
            for c in range(R // 8):
                rows = slice(8 * c, 8 * c + 8)
                for half, out in enumerate(outs):
                    tile = out[i * R + 8 * c : i * R + 8 * c + 8]
                    re, im = tile[:, :LANES], tile[:, LANES:]
                    for j, value in zip(range(3 * half, 3 * half + 3), (re + im, re, im)):
                        X[k, j, rows] = value
                        for t in range(T):
                            n, term = t * 6 + j, value * Y[t, j, rows]
                            sums[n] = term if c == 0 else sums[n] + term
            for t in range(T):
                for j in range(6):
                    acc[j, pl.ds(pl.multiple_of((t * K + k) * 8, 8), 8)] = sums[t * 6 + j]

    rows = T * K
    lane = lax.broadcasted_iota(jnp.int32, (rows, LANES), 1)

    def gathered(j):
        return functools.reduce(
            jnp.add, [acc[j, pl.ds(s, rows, stride=8)] for s in range(8)]
        )

    gathers = [gathered(j) for j in range(6)]
    cer, cei = joined(gathers[:3], lane == 0)
    cor, coi = joined(gathers[3:], None)
    total = jnp.concatenate([jnp.broadcast_to(v, (K, 1)) for v in totals], axis=0)
    base = cer[:, :1] * (1.0 / N) - total
    scale, edge = 2.0 / N, 1.0 / N
    ce = jnp.concatenate(
        [jnp.where(lane == 0, 0.0, cer * scale), cei * jnp.where(lane == 0, edge, scale)], axis=1
    )
    co = jnp.concatenate([cor * scale, coi * scale], axis=1)
    c_it.wait()
    u = mm3(ce, it[0], it[1])
    v = mm3(co, it[2], it[3])
    anneal = 4.0 / math.sqrt(R * N)
    low, high = anneal * (base + (u + v)), anneal * (base + (u - v))
    sc[:, :H] = low
    sc[:, H:] = high
    top = jnp.max(jnp.maximum(low, high), axis=1, keepdims=True)
    top = functools.reduce(jnp.maximum, [top[t * K : t * K + K] for t in range(T)])
    top_rows = jnp.concatenate([top] * T, axis=0)
    low, high = jnp.exp(low - top_rows), jnp.exp(high - top_rows)
    mass = jnp.sum(low + high, axis=1, keepdims=True)
    local = top + jnp.log(functools.reduce(jnp.add, [mass[t * K : t * K + K] for t in range(T)]))
    diagonal = lax.broadcasted_iota(jnp.int32, (K, LANES), 0) == lax.broadcasted_iota(
        jnp.int32, (K, LANES), 1
    )
    ls[rot] = jnp.sum(jnp.where(diagonal, local, 0.0), axis=0, keepdims=True)

    def tell(peer):
        pltpu.make_async_remote_copy(
            ls.at[rot], ls.at[rot], ls_sem.at[0], ls_sem.at[1],
            device_id=peer, device_id_type=MESH,
        ).start()

    def wait_rows(ref, n, sem):
        rows = ref.at[pl.ds(0, n)]
        pltpu.make_async_copy(rows, rows, sem).wait()

    def answer():
        return pltpu.make_async_remote_copy(
            fin.at[0], fin.at[0], fin_sem.at[0], fin_sem.at[1],
            device_id=at(0, 0, 1), device_id_type=MESH,
        )

    everyone = nz * nx

    @pl.when(lower)
    def _():
        pl.semaphore_wait(barrier, len(mine) + len(family))

    @pl.when(jnp.logical_not(lower))
    def _():
        pl.semaphore_wait(barrier, len(opposite) + len(family))
        tell(at(0, 0))

    for peer in mine:
        tell(peer)

    pe = mm3(low + high, ft[0], ft[1])
    po = mm3(low - high, ft[2], ft[3])

    @pl.when(lower)
    def _():
        wait_rows(ls, everyone - 1, ls_sem.at[1])
        each = ls[...]
        peak = jnp.max(each, axis=0)
        fin[0] = peak + jnp.log(jnp.sum(jnp.exp(each - peak), axis=0))
        answer().start()

    @pl.when(jnp.logical_not(lower))
    def _():
        answer().wait_recv()

    lse_row = fin[0]
    lse = jnp.sum(jnp.where(diagonal, lse_row, 0.0), axis=1, keepdims=True)
    factor = jnp.exp(top - lse)
    factor_rows = jnp.concatenate([factor] * T, axis=0)
    pe, po = pe * factor_rows, po * factor_rows
    spectra = three(pe[:, :LANES], pe[:, LANES:], lane == 0)
    spectra += three(po[:, :LANES], po[:, LANES:], None)
    for j in range(6):
        pb[j] = spectra[j]
    mass = mass * factor_rows
    weights = [jnp.sum(mass[t * K : t * K + K], axis=0, keepdims=True) for t in range(T)]
    lane = lax.broadcasted_iota(jnp.int32, (1, LANES), 1)
    wt[dp] = functools.reduce(jnp.add, [jnp.where(lane == t, weights[t], 0.0) for t in range(T)])

    first = lax.broadcasted_iota(jnp.int32, (8, LANES), 1) == 0

    def back(owner):
        sums = [[[None] * 6 for c in range(chunks)] for t in range(T)]
        for k in range(K):
            ps = [[pb[j, pl.ds(t * K + k, 8, stride=0)] for j in range(6)] for t in range(T)]
            for c in range(chunks):
                rows = pl.ds(pl.multiple_of(owner * share + 8 * c, 8), 8)
                for j in range(6):
                    x_ = X[k, j, rows]
                    for t in range(T):
                        term = x_ * ps[t][j]
                        sums[t][c][j] = term if k == 0 else sums[t][c][j] + term
        tiles = [None] * body
        for t in range(T):
            for c in range(chunks):
                parts = joined(sums[t][c][:3], first) + joined(sums[t][c][3:], None)
                for j in range(4):
                    tiles[c * half + t * 4 + j] = parts[j]
        return tiles

    order = (2, 1, 3, 0)

    def to_core(d):
        return pltpu.make_async_remote_copy(
            sa.at[d], ra.at[d], as_.at[d], ar.at[d],
            device_id=(y * 2 + 1 - core, rot), device_id_type=MESH,
        )

    def to_chip(n):
        return pltpu.make_async_remote_copy(
            sb.at[n], rb.at[n], bs.at[n], br.at[n],
            device_id=((y + (1 if n < 3 else ny - 1)) % ny * 2 + core, rot), device_id_type=MESH,
        )

    def send(n, tiles):
        for i, tile in enumerate(tiles):
            sb[n, i] = tile
        to_chip(n).start()

    def plus(tiles, n):
        to_chip(n).wait_recv()
        return [tile + rb[n, i] for i, tile in enumerate(tiles)]

    for d in order:
        for n, tile in enumerate(back((y + d) % ny * 2 + 1 - core)):
            sa[d, n] = tile
        to_core(d).start()
        if d == order[0]:
            for peer in family:
                pltpu.make_async_remote_copy(
                    wt.at[dp], wt.at[dp], wt_sem.at[0], wt_sem.at[1],
                    device_id=peer, device_id_type=MESH,
                ).start()

    def chip_sum(d):
        tiles = back((y + d) % ny * 2 + core)
        to_core(d).wait_recv()
        return [tile + ra[d, n] for n, tile in enumerate(tiles)]

    tiles = chip_sum(2)
    send(0, tiles[:half])
    send(3, tiles[half:])
    ahead = chip_sum(1)
    send(1, ahead[half:])
    behind = chip_sum(3)
    send(4, behind[:half])
    send(2, plus(ahead[:half], 0))
    send(5, plus(behind[half:], 3))
    tiles = chip_sum(0)

    scores = sc[...] - jnp.concatenate([lse] * T, axis=0)
    for t in range(T):
        for q in range(N // LANES):
            logp[pl.ds(q * T + t, K, stride=T * N // LANES)] = scores[
                t * K : t * K + K, q * LANES : (q + 1) * LANES
            ]

    tiles = plus(tiles[:half], 4) + plus(tiles[half:], 1)
    tiles = plus(tiles[:half], 2) + plus(tiles[half:], 5)
    family_rows = wt.at[pl.ds(0, len(family))]
    pltpu.make_async_copy(family_rows, family_rows, wt_sem.at[1]).wait()
    weight_row = jnp.sum(wt[...], axis=0) + 1.0
    parts = []
    for j in range(4):
        parts.append(
            jnp.concatenate(
                [tiles[c * half + t * 4 + j] for t in range(T) for c in range(chunks)], axis=0
            )
        )
    lane = lax.broadcasted_iota(jnp.int32, parts[0].shape, 1)
    ends = jnp.where(lane == 0, edge, scale)
    u = mm3(jnp.concatenate([parts[0] * ends, parts[1] * ends], axis=1), it[0], it[1])
    v = mm3(jnp.concatenate([parts[2] * scale, parts[3] * scale], axis=1), it[2], it[3])
    owned = pl.ds(pl.multiple_of(dp * share, 8), share)
    for t in range(T):
        rows = slice(t * share, (t + 1) * share)
        weight = weight_row[:, t : t + 1]
        new[t, :, :H] = (u[rows] + v[rows] + sl[t, owned, :H]) / weight
        new[t, :, H:] = (u[rows] - v[rows] + sl[t, owned, H:]) / weight

    wait_rows(ls, len(mine), ls_sem.at[0])

    @pl.when(lower)
    def _():
        answer().wait_send()

    @pl.when(jnp.logical_not(lower))
    def _():
        wait_rows(ls, 1, ls_sem.at[0])

    pltpu.make_async_copy(family_rows, family_rows, wt_sem.at[0]).wait()
    for d in order:
        to_core(d).wait_send()
    for n in range(6):
        to_chip(n).wait_send()


def hand_over(logp, new, logp_out, new_out, sem):
    copies = [
        pltpu.make_async_copy(logp, logp_out, sem.at[0]),
        pltpu.make_async_copy(new, new_out, sem.at[1]),
    ]
    for copy in copies:
        copy.start()
    for copy in copies:
        copy.wait()


def on_device(nx, frames, slices):
    K, R, N = frames.shape
    T = slices.shape[0]
    ny, nz = lax.axis_size("dp") // 2, lax.axis_size("rot") // nx
    assert ny == 4 and R // (2 * ny) == 16
    share = R // (2 * ny)
    body = T * 4 * (share // 8)
    forward, inverse = packed_tables(N)
    hbm = pl.BlockSpec(memory_space=pltpu.HBM)
    vmem = pl.BlockSpec(memory_space=pltpu.VMEM)
    dma = pltpu.SemaphoreType.DMA
    logp, new = pl.pallas_call(
        functools.partial(kernel, nx),
        out_shape=(
            jax.ShapeDtypeStruct((K * T * N // LANES, LANES), F32),
            jax.ShapeDtypeStruct((T, share, N), F32),
        ),
        in_specs=[hbm] * 4,
        out_specs=(vmem, vmem),
        scratch_shapes=[
            pltpu.VMEM((K, R, N), jnp.int32),
            pltpu.VMEM((T, R, N), F32),
            pltpu.VMEM((4, N // 2, N // 2), BF16),
            pltpu.VMEM((4, N // 2, N // 2), BF16),
            pltpu.VMEM((K, 6, R, LANES), F32),
            pltpu.VMEM((T, 6, R, LANES), F32),
            pltpu.VMEM((6, 8 * T * K, LANES), F32),
            pltpu.VMEM((6, T * K, LANES), F32),
            pltpu.VMEM((T * K, N), F32),
            pltpu.VMEM((nx * nz, 1, LANES), F32),
            pltpu.VMEM((1, 1, LANES), F32),
            pltpu.VMEM((2 * ny, 1, LANES), F32),
            pltpu.VMEM((ny, body, 8, LANES), F32),
            pltpu.VMEM((ny, body, 8, LANES), F32),
            pltpu.VMEM((6, body // 2, 8, LANES), F32),
            pltpu.VMEM((6, body // 2, 8, LANES), F32),
            dma((K // GROUP,)),
            dma((3,)),
            dma((2,)),
            dma((2,)),
            dma((2,)),
            dma((ny,)),
            dma((ny,)),
            dma((6,)),
            dma((6,)),
        ],
        compiler_params=pltpu.CompilerParams(
            collective_id=0, has_side_effects=True, vmem_limit_bytes=32 << 20
        ),
    )(*(pltpu.with_memory_space_constraint(v, pltpu.HBM) for v in (frames, slices, jnp.asarray(forward), jnp.asarray(inverse))))
    logp, new = pl.pallas_call(
        hand_over,
        out_shape=(
            jax.ShapeDtypeStruct(logp.shape, F32),
            jax.ShapeDtypeStruct(new.shape, F32),
        ),
        in_specs=[vmem, vmem],
        out_specs=(hbm, hbm),
        scratch_shapes=[dma((2,))],
        compiler_params=pltpu.CompilerParams(vmem_limit_bytes=1 << 20),
    )(logp, new)
    log_resp = logp.reshape(K, N // LANES, T, LANES).transpose(0, 2, 1, 3).reshape(K, T, N)
    return log_resp, new


def solution(mesh, nx=4):
    in_specs = (P("dp", None, None), P("rot", None, None))
    out_specs = (P("dp", "rot", None), P("rot", "dp", None))
    return jax.shard_map(
        functools.partial(on_device, nx),
        mesh=mesh, in_specs=in_specs, out_specs=out_specs, check_vma=False,
    )
```

```python
import functools
import math

import jax
import jax.numpy as jnp
import numpy as np
from jax import lax
from jax.experimental import pallas as pl
from jax.experimental.pallas import tpu as pltpu
from jax.sharding import PartitionSpec as P

F32, BF16 = jnp.float32, jnp.bfloat16
MESH = pl.DeviceIdType.MESH
LANES = 128
GROUP = 4


def packed_tables(angles):
    half, quarter = angles // 2, angles // 4
    p, g = np.arange(half)[:, None], np.arange(quarter)[None, :]
    even_phase = 2.0 * np.pi * ((p * g) % half) / half
    even = np.concatenate([np.cos(even_phase), -np.sin(even_phase)], axis=1)
    even[:, quarter] = 1.0 - 2.0 * (np.arange(half) % 2)
    odd_phase = 2.0 * np.pi * ((p * (2 * g + 1)) % angles) / angles
    odd = np.concatenate([np.cos(odd_phase), -np.sin(odd_phase)], axis=1)
    parts = []
    for table in (even, odd):
        high = table.astype(BF16)
        parts += [high, (table - high.astype(np.float64)).astype(BF16)]
    forward = np.stack(parts)
    return forward, np.ascontiguousarray(forward.transpose(0, 2, 1))


def mm(a, b):
    return jnp.dot(a, b, preferred_element_type=F32)


def split(x):
    high = x.astype(BF16)
    return high, (x - high.astype(F32)).astype(BF16)


def mm3(x, high, low):
    return mm_parts(split(x), high, low)


def mm_parts(parts, high, low):
    rows = parts[0].shape[0]
    stacked = mm(jnp.concatenate(parts, axis=0), high)
    total = mm(parts[0], low)
    for i in reversed(range(len(parts))):
        total = total + stacked[i * rows : (i + 1) * rows]
    return total


def three(re, im, first):
    if first is None:
        return re, re + im, re - im
    return re, jnp.where(first, re, re + im), jnp.where(first, im, re - im)


def joined(sums, first):
    one, two, last = sums
    re, im = one - last, one - two
    if first is None:
        return re, im
    return jnp.where(first, two, re), jnp.where(first, last, im)


def lse_of_rows(rows):
    peak = jnp.max(rows, axis=0)
    return peak + jnp.log(jnp.sum(jnp.exp(rows - peak), axis=0))


def kernel(
    nx, frames, slices, ftab_hbm, itab_hbm, logp, new,
    fr, sl, ft, it, X, Y, acc, pb, sc, ls, fin, wt, kept, sa, ra, sb, rb,
    fsem, msem, ls_sem, fin_sem, wt_sem, as_, ar, bs, br,
):
    K, R, N = fr.shape
    T, H = sl.shape[0], N // 2
    dp, rot = lax.axis_index("dp"), lax.axis_index("rot")
    ny, nz = lax.axis_size("dp") // 2, lax.axis_size("rot") // nx
    y, core = dp // 2, dp % 2
    z, x = rot // nx, rot % nx
    share = R // (2 * ny)
    chunks, half = share // 8, T * 4
    body = half * chunks

    c_ft = pltpu.make_async_copy(ftab_hbm, ft, msem.at[0])
    c_sl = pltpu.make_async_copy(slices, sl, msem.at[1])
    c_it = pltpu.make_async_copy(itab_hbm, it, msem.at[2])
    for i in range(4):
        for t in range(T):
            part = pl.ds(i * R // 4, R // 4)
            pltpu.make_async_copy(slices.at[t, part], sl.at[t, part], msem.at[1]).start()
        pltpu.make_async_copy(ftab_hbm.at[i], ft.at[i], msem.at[0]).start()

    def group_copy(g):
        part = pl.ds(g * GROUP, GROUP)
        return pltpu.make_async_copy(frames.at[part], fr.at[part], fsem.at[g])

    barrier = pltpu.get_barrier_semaphore()
    low_z = nz // 2
    lower = z < low_z
    steps = [(i, j) for i in range(low_z) for j in range(nx)]
    steps.sort(key=lambda s: -(min(s[0], low_z - s[0]) + min(s[1], nx - s[1])))

    def at(i, j, upper=0):
        return dp, ((z + i) % low_z + upper * low_z) * nx + (x + j) % nx

    mine = [at(i, j) for i, j in steps if i or j]
    opposite = [at(i, j, 1) for i, j in steps]
    family = [((dp + d) % (2 * ny), rot) for d in range(1, 2 * ny)]
    def signal(peer):
        pl.semaphore_signal(barrier, inc=1, device_id=peer, device_id_type=MESH)

    @pl.when(lower)
    def _():
        for peer in opposite + mine:
            signal(peer)

    for peer in family:
        signal(peer)

    @pl.loop(0, K)
    def _(k):
        pltpu.make_async_copy(frames.at[k], fr.at[k], fsem.at[k // GROUP]).start()

    c_it.start()

    c_sl.wait()
    c_ft.wait()
    first = lax.broadcasted_iota(jnp.int32, (R, LANES), 1) == 0
    totals = []
    for t in range(T):
        values = sl[t]
        totals.append(jnp.sum(jnp.sum(values, axis=0, keepdims=True), axis=1, keepdims=True))
        logs = jnp.log(values)
        even, odd = logs[:, :H] + logs[:, H:], logs[:, :H] - logs[:, H:]
        eh, em = split(even)
        el = (even - eh.astype(F32) - em.astype(F32)).astype(BF16)
        ye = mm_parts((eh, em, el), ft[0], ft[1])
        yo = mm3(odd, ft[2], ft[3])
        pairs = three(ye[:, :LANES], ye[:, LANES:], first)
        pairs += three(yo[:, :LANES], yo[:, LANES:], None)
        for j in range(6):
            Y[t, j] = pairs[j]

    @pl.loop(0, K // GROUP)
    def _(g):
        group_copy(g).wait()
        part = pl.ds(g * GROUP, GROUP)
        left = fr[part, :, :H].astype(F32).astype(BF16).reshape(GROUP * R, H)
        right = fr[part, :, H:].astype(F32).astype(BF16).reshape(GROUP * R, H)
        outs = mm(left + right, ft[0]), mm(left - right, ft[2])
        for i in range(GROUP):
            k = g * GROUP + i
            sums = [None] * (6 * T)
            for c in range(R // 8):
                rows = slice(8 * c, 8 * c + 8)
                for half, out in enumerate(outs):
                    tile = out[i * R + 8 * c : i * R + 8 * c + 8]
                    re, im = tile[:, :LANES], tile[:, LANES:]
                    for j, value in zip(range(3 * half, 3 * half + 3), (re + im, re, im)):
                        X[k, j, rows] = value
                        for t in range(T):
                            n, term = t * 6 + j, value * Y[t, j, rows]
                            sums[n] = term if c == 0 else sums[n] + term
            for t in range(T):
                for j in range(6):
                    acc[j, pl.ds(pl.multiple_of((t * K + k) * 8, 8), 8)] = sums[t * 6 + j]

    rows = T * K
    lane = lax.broadcasted_iota(jnp.int32, (rows, LANES), 1)

    def gathered(j):
        return functools.reduce(
            jnp.add, [acc[j, pl.ds(s, rows, stride=8)] for s in range(8)]
        )

    gathers = [gathered(j) for j in range(6)]
    cer, cei = joined(gathers[:3], lane == 0)
    cor, coi = joined(gathers[3:], None)
    total = jnp.concatenate([jnp.broadcast_to(v, (K, 1)) for v in totals], axis=0)
    base = cer[:, :1] * (1.0 / N) - total
    scale, edge = 2.0 / N, 1.0 / N
    ce = jnp.concatenate(
        [jnp.where(lane == 0, 0.0, cer * scale), cei * jnp.where(lane == 0, edge, scale)], axis=1
    )
    co = jnp.concatenate([cor * scale, coi * scale], axis=1)
    c_it.wait()
    u = mm3(ce, it[0], it[1])
    v = mm3(co, it[2], it[3])
    anneal = 4.0 / math.sqrt(R * N)
    low, high = anneal * (base + (u + v)), anneal * (base + (u - v))
    sc[:, :H] = low
    sc[:, H:] = high
    top = jnp.max(jnp.maximum(low, high), axis=1, keepdims=True)
    top = functools.reduce(jnp.maximum, [top[t * K : t * K + K] for t in range(T)])
    top_rows = jnp.concatenate([top] * T, axis=0)
    low, high = jnp.exp(low - top_rows), jnp.exp(high - top_rows)
    mass = jnp.sum(low + high, axis=1, keepdims=True)
    local = top + jnp.log(functools.reduce(jnp.add, [mass[t * K : t * K + K] for t in range(T)]))
    diagonal = lax.broadcasted_iota(jnp.int32, (K, LANES), 0) == lax.broadcasted_iota(
        jnp.int32, (K, LANES), 1
    )
    ls[rot] = jnp.sum(jnp.where(diagonal, local, 0.0), axis=0, keepdims=True)

    def tell(peer):
        pltpu.make_async_remote_copy(
            ls.at[rot], ls.at[rot], ls_sem.at[0], ls_sem.at[1 + z // low_z],
            device_id=peer, device_id_type=MESH,
        ).start()

    def wait_rows(ref, n, sem):
        rows = ref.at[pl.ds(0, n)]
        pltpu.make_async_copy(rows, rows, sem).wait()

    def answer():
        return pltpu.make_async_remote_copy(
            fin.at[0], fin.at[0], fin_sem.at[0], fin_sem.at[1],
            device_id=at(0, 0, 1), device_id_type=MESH,
        )

    everyone = nz * nx

    @pl.when(lower)
    def _():
        pl.semaphore_wait(barrier, len(mine) + len(family))

    @pl.when(jnp.logical_not(lower))
    def _():
        pl.semaphore_wait(barrier, len(opposite) + len(family))
        tell(at(0, 0))

    for peer in mine:
        tell(peer)

    pe = mm3(low + high, ft[0], ft[1])
    po = mm3(low - high, ft[2], ft[3])

    @pl.when(lower)
    def _():
        wait_rows(ls, len(mine), ls_sem.at[1])
        near_row = lse_of_rows(ls[: everyone // 2])
        wait_rows(ls, everyone // 2, ls_sem.at[2])
        far_row = lse_of_rows(ls[everyone // 2 :])
        peak = jnp.maximum(near_row, far_row)
        fin[0] = peak + jnp.log(jnp.exp(near_row - peak) + jnp.exp(far_row - peak))
        answer().start()

    @pl.when(jnp.logical_not(lower))
    def _():
        answer().wait_recv()

    lse_row = fin[0]
    lse = jnp.sum(jnp.where(diagonal, lse_row, 0.0), axis=1, keepdims=True)
    factor = jnp.exp(top - lse)
    factor_rows = jnp.concatenate([factor] * T, axis=0)
    pe, po = pe * factor_rows, po * factor_rows
    spectra = three(pe[:, :LANES], pe[:, LANES:], lane == 0)
    spectra += three(po[:, :LANES], po[:, LANES:], None)
    for j in range(6):
        pb[j] = spectra[j]
    mass = mass * factor_rows
    weights = [jnp.sum(mass[t * K : t * K + K], axis=0, keepdims=True) for t in range(T)]
    lane = lax.broadcasted_iota(jnp.int32, (1, LANES), 1)
    wt[dp] = functools.reduce(jnp.add, [jnp.where(lane == t, weights[t], 0.0) for t in range(T)])

    first = lax.broadcasted_iota(jnp.int32, (8, LANES), 1) == 0

    def back(owner):
        sums = [[[None] * 6 for c in range(chunks)] for t in range(T)]
        for k in range(K):
            ps = [[pb[j, pl.ds(t * K + k, 8, stride=0)] for j in range(6)] for t in range(T)]
            for c in range(chunks):
                rows = pl.ds(pl.multiple_of(owner * share + 8 * c, 8), 8)
                for j in range(6):
                    x_ = X[k, j, rows]
                    for t in range(T):
                        term = x_ * ps[t][j]
                        sums[t][c][j] = term if k == 0 else sums[t][c][j] + term
        tiles = [None] * body
        for t in range(T):
            for c in range(chunks):
                parts = joined(sums[t][c][:3], first) + joined(sums[t][c][3:], None)
                for j in range(4):
                    tiles[c * half + t * 4 + j] = parts[j]
        return tiles

    order = (2, 1, 3, 0)

    def to_core(d):
        return pltpu.make_async_remote_copy(
            sa.at[d], ra.at[d], as_.at[d], ar.at[d],
            device_id=(y * 2 + 1 - core, rot), device_id_type=MESH,
        )

    def to_chip(n, p):
        piece = pl.ds(p * half // 2, half // 2)
        return pltpu.make_async_remote_copy(
            sb.at[n, piece], rb.at[n, piece], bs.at[2 * n + p], br.at[2 * n + p],
            device_id=((y + (1 if n < 3 else ny - 1)) % ny * 2 + core, rot), device_id_type=MESH,
        )

    def send_piece(n, p, tiles):
        for i, tile in enumerate(tiles):
            sb[n, p * half // 2 + i] = tile
        to_chip(n, p).start()

    def send(n, tiles):
        for p in range(2):
            send_piece(n, p, tiles[p * half // 2 : (p + 1) * half // 2])

    def plus_piece(tiles, n, p):
        to_chip(n, p).wait_recv()
        return [tile + rb[n, p * half // 2 + i] for i, tile in enumerate(tiles)]

    def plus(tiles, n):
        return plus_piece(tiles[: half // 2], n, 0) + plus_piece(tiles[half // 2 :], n, 1)

    def give(d):
        for n, tile in enumerate(back((y + d) % ny * 2 + 1 - core)):
            sa[d, n] = tile
        to_core(d).start()

    def chip_sum(d):
        tiles = back((y + d) % ny * 2 + core)
        to_core(d).wait_recv()
        return [tile + ra[d, n] for n, tile in enumerate(tiles)]

    def give_on(which, ds):
        @pl.when(core == which)
        def _():
            for d in ds:
                give(d)

    give(2)
    for peer in family:
        pltpu.make_async_remote_copy(
            wt.at[dp], wt.at[dp], wt_sem.at[0], wt_sem.at[1],
            device_id=peer, device_id_type=MESH,
        ).start()
    give_on(1, (1, 3, 0))
    tiles = chip_sum(2)
    send(0, tiles[:half])
    send(3, tiles[half:])
    give_on(0, (1, 3, 0))
    ahead = chip_sum(1)
    send(1, ahead[half:])
    for n in range(half):
        kept[0, n] = ahead[n]
    behind = chip_sum(3)
    send(4, behind[:half])
    for n in range(half):
        kept[1, n] = behind[half + n]
    for p in range(2):
        for i, came, goes in ((0, 0, 2), (1, 3, 5)):
            piece = [kept[i, p * half // 2 + n] for n in range(half // 2)]
            send_piece(goes, p, plus_piece(piece, came, p))
    tiles = chip_sum(0)

    scores = sc[...] - jnp.concatenate([lse] * T, axis=0)
    for t in range(T):
        for q in range(N // LANES):
            logp[pl.ds(q * T + t, K, stride=T * N // LANES)] = scores[
                t * K : t * K + K, q * LANES : (q + 1) * LANES
            ]

    tiles = plus(tiles[:half], 4) + plus(tiles[half:], 1)
    tiles = plus(tiles[:half], 2) + plus(tiles[half:], 5)
    family_rows = wt.at[pl.ds(0, len(family))]
    pltpu.make_async_copy(family_rows, family_rows, wt_sem.at[1]).wait()
    weight_row = jnp.sum(wt[...], axis=0) + 1.0
    parts = []
    for j in range(4):
        parts.append(
            jnp.concatenate(
                [tiles[c * half + t * 4 + j] for t in range(T) for c in range(chunks)], axis=0
            )
        )
    lane = lax.broadcasted_iota(jnp.int32, parts[0].shape, 1)
    ends = jnp.where(lane == 0, edge, scale)
    u = mm3(jnp.concatenate([parts[0] * ends, parts[1] * ends], axis=1), it[0], it[1])
    v = mm3(jnp.concatenate([parts[2] * scale, parts[3] * scale], axis=1), it[2], it[3])
    owned = pl.ds(pl.multiple_of(dp * share, 8), share)
    for t in range(T):
        rows = slice(t * share, (t + 1) * share)
        weight = weight_row[:, t : t + 1]
        new[t, :, :H] = (u[rows] + v[rows] + sl[t, owned, :H]) / weight
        new[t, :, H:] = (u[rows] - v[rows] + sl[t, owned, H:]) / weight

    wait_rows(ls, len(mine), ls_sem.at[0])

    @pl.when(lower)
    def _():
        answer().wait_send()

    @pl.when(jnp.logical_not(lower))
    def _():
        wait_rows(ls, 1, ls_sem.at[0])

    pltpu.make_async_copy(family_rows, family_rows, wt_sem.at[0]).wait()
    for d in order:
        to_core(d).wait_send()
    for n in range(6):
        for p in range(2):
            to_chip(n, p).wait_send()


def hand_over(logp, new, logp_out, new_out, sem):
    copies = [
        pltpu.make_async_copy(logp, logp_out, sem.at[0]),
        pltpu.make_async_copy(new, new_out, sem.at[1]),
    ]
    for copy in copies:
        copy.start()
    for copy in copies:
        copy.wait()


def on_device(nx, frames, slices):
    K, R, N = frames.shape
    T = slices.shape[0]
    ny, nz = lax.axis_size("dp") // 2, lax.axis_size("rot") // nx
    assert ny == 4 and R // (2 * ny) == 16
    share = R // (2 * ny)
    body = T * 4 * (share // 8)
    forward, inverse = packed_tables(N)
    hbm = pl.BlockSpec(memory_space=pltpu.HBM)
    vmem = pl.BlockSpec(memory_space=pltpu.VMEM)
    dma = pltpu.SemaphoreType.DMA
    logp, new = pl.pallas_call(
        functools.partial(kernel, nx),
        out_shape=(
            jax.ShapeDtypeStruct((K * T * N // LANES, LANES), F32),
            jax.ShapeDtypeStruct((T, share, N), F32),
        ),
        in_specs=[hbm] * 4,
        out_specs=(vmem, vmem),
        scratch_shapes=[
            pltpu.VMEM((K, R, N), jnp.int32),
            pltpu.VMEM((T, R, N), F32),
            pltpu.VMEM((4, N // 2, N // 2), BF16),
            pltpu.VMEM((4, N // 2, N // 2), BF16),
            pltpu.VMEM((K, 6, R, LANES), F32),
            pltpu.VMEM((T, 6, R, LANES), F32),
            pltpu.VMEM((6, 8 * T * K, LANES), F32),
            pltpu.VMEM((6, T * K, LANES), F32),
            pltpu.VMEM((T * K, N), F32),
            pltpu.VMEM((nx * nz, 1, LANES), F32),
            pltpu.VMEM((1, 1, LANES), F32),
            pltpu.VMEM((2 * ny, 1, LANES), F32),
            pltpu.VMEM((2, body // 2, 8, LANES), F32),
            pltpu.VMEM((ny, body, 8, LANES), F32),
            pltpu.VMEM((ny, body, 8, LANES), F32),
            pltpu.VMEM((6, body // 2, 8, LANES), F32),
            pltpu.VMEM((6, body // 2, 8, LANES), F32),
            dma((K // GROUP,)),
            dma((3,)),
            dma((3,)),
            dma((2,)),
            dma((2,)),
            dma((ny,)),
            dma((ny,)),
            dma((12,)),
            dma((12,)),
        ],
        compiler_params=pltpu.CompilerParams(
            collective_id=0, has_side_effects=True, vmem_limit_bytes=32 << 20
        ),
    )(*(pltpu.with_memory_space_constraint(v, pltpu.HBM) for v in (frames, slices, jnp.asarray(forward), jnp.asarray(inverse))))
    logp, new = pl.pallas_call(
        hand_over,
        out_shape=(
            jax.ShapeDtypeStruct(logp.shape, F32),
            jax.ShapeDtypeStruct(new.shape, F32),
        ),
        in_specs=[vmem, vmem],
        out_specs=(hbm, hbm),
        scratch_shapes=[dma((2,))],
        compiler_params=pltpu.CompilerParams(vmem_limit_bytes=1 << 20),
    )(logp, new)
    log_resp = logp.reshape(K, N // LANES, T, LANES).transpose(0, 2, 1, 3).reshape(K, T, N)
    return log_resp, new


def solution(mesh, nx=4):
    in_specs = (P("dp", None, None), P("rot", None, None))
    out_specs = (P("dp", "rot", None), P("rot", "dp", None))
    return jax.shard_map(
        functools.partial(on_device, nx),
        mesh=mesh, in_specs=in_specs, out_specs=out_specs, check_vma=False,
    )
```

```python
import functools
import math

import jax
import jax.numpy as jnp
import numpy as np
from jax import lax
from jax.experimental import pallas as pl
from jax.experimental.pallas import tpu as pltpu
from jax.sharding import PartitionSpec as P

F32, BF16 = jnp.float32, jnp.bfloat16
MESH = pl.DeviceIdType.MESH
LANES = 128
GROUP = 4


def packed_tables(angles):
    half, quarter = angles // 2, angles // 4
    p, g = np.arange(half)[:, None], np.arange(quarter)[None, :]
    even_phase = 2.0 * np.pi * ((p * g) % half) / half
    even = np.concatenate([np.cos(even_phase), -np.sin(even_phase)], axis=1)
    even[:, quarter] = 1.0 - 2.0 * (np.arange(half) % 2)
    odd_phase = 2.0 * np.pi * ((p * (2 * g + 1)) % angles) / angles
    odd = np.concatenate([np.cos(odd_phase), -np.sin(odd_phase)], axis=1)
    parts = []
    for table in (even, odd):
        high = table.astype(BF16)
        parts += [high, (table - high.astype(np.float64)).astype(BF16)]
    return np.stack(parts)[:, : half // 2]


def mm(a, b, axis=0):
    return lax.dot_general(a, b, (((1,), (axis,)), ((), ())), preferred_element_type=F32)


def split(x):
    high = x.astype(BF16)
    return high, (x - high.astype(F32)).astype(BF16)


def mm3(x, high, low, axis=0):
    return mm_parts(split(x), high, low, axis)


def mm_parts(parts, high, low, axis=0):
    rows = parts[0].shape[0]
    stacked = mm(jnp.concatenate(parts, axis=0), high, axis)
    total = mm(parts[0], low, axis)
    for i in reversed(range(len(parts))):
        total = total + stacked[i * rows : (i + 1) * rows]
    return total


def three(re, im, first):
    if first is None:
        return re, re + im, re - im
    return re, jnp.where(first, re, re + im), jnp.where(first, im, re - im)


def joined(sums, first):
    one, two, last = sums
    re, im = one - last, one - two
    if first is None:
        return re, im
    return jnp.where(first, two, re), jnp.where(first, last, im)


def lse_of_rows(rows):
    peak = jnp.max(rows, axis=0)
    return peak + jnp.log(jnp.sum(jnp.exp(rows - peak), axis=0))


def kernel(
    nx, frames, slices, ftab_hbm, logp, new,
    fr, sl, ft, X, Y, acc, pb, sc, ls, fin, wt, kept, sa, ra, sb, rb,
    fsem, msem, ls_sem, fin_sem, wt_sem, as_, ar, bs, br,
):
    K, R, N = fr.shape
    T, H = sl.shape[0], N // 2
    dp, rot = lax.axis_index("dp"), lax.axis_index("rot")
    ny, nz = lax.axis_size("dp") // 2, lax.axis_size("rot") // nx
    y, core = dp // 2, dp % 2
    z, x = rot // nx, rot % nx
    share = R // (2 * ny)
    chunks, half = share // 8, T * 4
    body = half * chunks

    quarter = H // 2
    c_ft = pltpu.make_async_copy(ftab_hbm, ft.at[:, pl.ds(0, quarter)], msem.at[0])
    c_sl = pltpu.make_async_copy(slices, sl, msem.at[1])
    for i in range(4):
        for t in range(T):
            part = pl.ds(i * R // 4, R // 4)
            pltpu.make_async_copy(slices.at[t, part], sl.at[t, part], msem.at[1]).start()
        pltpu.make_async_copy(
            ftab_hbm.at[i], ft.at[i, pl.ds(0, quarter)], msem.at[0]
        ).start()

    def group_copy(g):
        part = pl.ds(g * GROUP, GROUP)
        return pltpu.make_async_copy(frames.at[part], fr.at[part], fsem.at[g])

    barrier = pltpu.get_barrier_semaphore()
    low_z = nz // 4
    lower = z < low_z
    steps = [(i, j) for i in range(low_z) for j in range(nx)]
    steps.sort(key=lambda s: -(min(s[0], low_z - s[0]) + min(s[1], nx - s[1])))

    def at(i, j, upper=0):
        return dp, ((z + i) % low_z + upper * low_z) * nx + (x + j) % nx

    mine = [at(i, j) for i, j in steps if i or j]
    opposite = [at(i, j, u) for u in (2, 3, 1) for i, j in steps]
    family = [((dp + d) % (2 * ny), rot) for d in range(1, 2 * ny)]
    def signal(peer):
        pl.semaphore_signal(barrier, inc=1, device_id=peer, device_id_type=MESH)

    @pl.when(lower)
    def _():
        for peer in opposite + mine:
            signal(peer)

    for peer in family:
        signal(peer)

    @pl.loop(0, K)
    def _(k):
        pltpu.make_async_copy(frames.at[k], fr.at[k], fsem.at[k // GROUP]).start()


    c_ft.wait()
    turn = lax.broadcasted_iota(jnp.int32, (quarter, LANES), 1) % 2
    turn = (1 - 2 * turn).astype(F32).astype(BF16)
    for i in range(4):
        cosine, sine = ft[i, :quarter, :LANES], ft[i, :quarter, LANES:]
        if i >= 2:
            cosine, sine = sine, -cosine
        ft[i, quarter:, :LANES] = cosine * turn
        ft[i, quarter:, LANES:] = sine * turn
    c_sl.wait()
    first = lax.broadcasted_iota(jnp.int32, (R, LANES), 1) == 0
    totals = []
    for t in range(T):
        values = sl[t]
        totals.append(jnp.sum(jnp.sum(values, axis=0, keepdims=True), axis=1, keepdims=True))
        logs = jnp.log(values)
        even, odd = logs[:, :H] + logs[:, H:], logs[:, :H] - logs[:, H:]
        eh, em = split(even)
        el = (even - eh.astype(F32) - em.astype(F32)).astype(BF16)
        ye = mm_parts((eh, em, el), ft[0], ft[1])
        yo = mm3(odd, ft[2], ft[3])
        pairs = three(ye[:, :LANES], ye[:, LANES:], first)
        pairs += three(yo[:, :LANES], yo[:, LANES:], None)
        for j in range(6):
            Y[t, j] = pairs[j]

    @pl.loop(0, K // GROUP)
    def _(g):
        group_copy(g).wait()
        part = pl.ds(g * GROUP, GROUP)
        left = fr[part, :, :H].astype(F32).astype(BF16).reshape(GROUP * R, H)
        right = fr[part, :, H:].astype(F32).astype(BF16).reshape(GROUP * R, H)
        outs = mm(left + right, ft[0]), mm(left - right, ft[2])
        for i in range(GROUP):
            k = g * GROUP + i
            sums = [None] * (6 * T)
            for c in range(R // 8):
                rows = slice(8 * c, 8 * c + 8)
                for half, out in enumerate(outs):
                    tile = out[i * R + 8 * c : i * R + 8 * c + 8]
                    re, im = tile[:, :LANES], tile[:, LANES:]
                    for j, value in zip(range(3 * half, 3 * half + 3), (re + im, re, im)):
                        X[k, j, rows] = value
                        for t in range(T):
                            n, term = t * 6 + j, value * Y[t, j, rows]
                            sums[n] = term if c == 0 else sums[n] + term
            for t in range(T):
                for j in range(6):
                    acc[j, pl.ds(pl.multiple_of((t * K + k) * 8, 8), 8)] = sums[t * 6 + j]

    rows = T * K
    lane = lax.broadcasted_iota(jnp.int32, (rows, LANES), 1)

    def gathered(j):
        return functools.reduce(
            jnp.add, [acc[j, pl.ds(s, rows, stride=8)] for s in range(8)]
        )

    gathers = [gathered(j) for j in range(6)]
    cer, cei = joined(gathers[:3], lane == 0)
    cor, coi = joined(gathers[3:], None)
    total = jnp.concatenate([jnp.broadcast_to(v, (K, 1)) for v in totals], axis=0)
    base = cer[:, :1] * (1.0 / N) - total
    scale, edge = 2.0 / N, 1.0 / N
    ce = jnp.concatenate(
        [jnp.where(lane == 0, 0.0, cer * scale), cei * jnp.where(lane == 0, edge, scale)], axis=1
    )
    co = jnp.concatenate([cor * scale, coi * scale], axis=1)
    u = mm3(ce, ft[0], ft[1], 1)
    v = mm3(co, ft[2], ft[3], 1)
    anneal = 4.0 / math.sqrt(R * N)
    low, high = anneal * (base + (u + v)), anneal * (base + (u - v))
    sc[:, :H] = low
    sc[:, H:] = high
    top = jnp.max(jnp.maximum(low, high), axis=1, keepdims=True)
    top = functools.reduce(jnp.maximum, [top[t * K : t * K + K] for t in range(T)])
    top_rows = jnp.concatenate([top] * T, axis=0)
    low, high = jnp.exp(low - top_rows), jnp.exp(high - top_rows)
    mass = jnp.sum(low + high, axis=1, keepdims=True)
    local = top + jnp.log(functools.reduce(jnp.add, [mass[t * K : t * K + K] for t in range(T)]))
    diagonal = lax.broadcasted_iota(jnp.int32, (K, LANES), 0) == lax.broadcasted_iota(
        jnp.int32, (K, LANES), 1
    )
    ls[rot] = jnp.sum(jnp.where(diagonal, local, 0.0), axis=0, keepdims=True)

    def tell(peer):
        pltpu.make_async_remote_copy(
            ls.at[rot], ls.at[rot], ls_sem.at[0], ls_sem.at[2 - lower.astype(jnp.int32)],
            device_id=peer, device_id_type=MESH,
        ).start()

    def wait_rows(ref, n, sem):
        rows = ref.at[pl.ds(0, n)]
        pltpu.make_async_copy(rows, rows, sem).wait()

    def answer(u):
        return pltpu.make_async_remote_copy(
            fin.at[0], fin.at[0], fin_sem.at[0], fin_sem.at[1],
            device_id=at(0, 0, u), device_id_type=MESH,
        )

    everyone = nz * nx

    @pl.when(lower)
    def _():
        pl.semaphore_wait(barrier, len(mine) + len(family))

    @pl.when(jnp.logical_not(lower))
    def _():
        pl.semaphore_wait(barrier, len(steps) + len(family))
        tell(at(0, 0))

    for peer in mine:
        tell(peer)

    pe = mm3(low + high, ft[0], ft[1])
    po = mm3(low - high, ft[2], ft[3])

    @pl.when(lower)
    def _():
        wait_rows(ls, len(mine), ls_sem.at[1])
        near_row = lse_of_rows(ls[: len(steps)])
        wait_rows(ls, len(opposite), ls_sem.at[2])
        far_row = lse_of_rows(ls[len(steps) :])
        peak = jnp.maximum(near_row, far_row)
        fin[0] = peak + jnp.log(jnp.exp(near_row - peak) + jnp.exp(far_row - peak))
        for u in (2, 3, 1):
            answer(u).start()

    @pl.when(jnp.logical_not(lower))
    def _():
        wait_rows(fin, 1, fin_sem.at[1])

    lse_row = fin[0]
    lse = jnp.sum(jnp.where(diagonal, lse_row, 0.0), axis=1, keepdims=True)
    factor = jnp.exp(top - lse)
    factor_rows = jnp.concatenate([factor] * T, axis=0)
    pe, po = pe * factor_rows, po * factor_rows
    spectra = three(pe[:, :LANES], pe[:, LANES:], lane == 0)
    spectra += three(po[:, :LANES], po[:, LANES:], None)
    for j in range(6):
        pb[j] = spectra[j]
    mass = mass * factor_rows
    weights = [jnp.sum(mass[t * K : t * K + K], axis=0, keepdims=True) for t in range(T)]
    lane = lax.broadcasted_iota(jnp.int32, (1, LANES), 1)
    wt[dp] = functools.reduce(jnp.add, [jnp.where(lane == t, weights[t], 0.0) for t in range(T)])

    first = lax.broadcasted_iota(jnp.int32, (8, LANES), 1) == 0

    def back(owner):
        sums = [[[None] * 6 for c in range(chunks)] for t in range(T)]
        for k in range(K):
            ps = [[pb[j, pl.ds(t * K + k, 8, stride=0)] for j in range(6)] for t in range(T)]
            for c in range(chunks):
                rows = pl.ds(pl.multiple_of(owner * share + 8 * c, 8), 8)
                for j in range(6):
                    x_ = X[k, j, rows]
                    for t in range(T):
                        term = x_ * ps[t][j]
                        sums[t][c][j] = term if k == 0 else sums[t][c][j] + term
        tiles = [None] * body
        for t in range(T):
            for c in range(chunks):
                parts = joined(sums[t][c][:3], first) + joined(sums[t][c][3:], None)
                for j in range(4):
                    tiles[c * half + t * 4 + j] = parts[j]
        return tiles

    order = (2, 1, 3, 0)

    def to_core(d):
        return pltpu.make_async_remote_copy(
            sa.at[d], ra.at[d], as_.at[d], ar.at[d],
            device_id=(y * 2 + 1 - core, rot), device_id_type=MESH,
        )

    def to_chip(n, p):
        piece = pl.ds(p * half // 2, half // 2)
        return pltpu.make_async_remote_copy(
            sb.at[n, piece], rb.at[n, piece], bs.at[2 * n + p], br.at[2 * n + p],
            device_id=((y + (1 if n < 3 else ny - 1)) % ny * 2 + core, rot), device_id_type=MESH,
        )

    def send_piece(n, p, tiles):
        for i, tile in enumerate(tiles):
            sb[n, p * half // 2 + i] = tile
        to_chip(n, p).start()

    def send(n, tiles):
        for p in range(2):
            send_piece(n, p, tiles[p * half // 2 : (p + 1) * half // 2])

    def plus_piece(tiles, n, p):
        to_chip(n, p).wait_recv()
        return [tile + rb[n, p * half // 2 + i] for i, tile in enumerate(tiles)]

    def plus(tiles, n):
        return plus_piece(tiles[: half // 2], n, 0) + plus_piece(tiles[half // 2 :], n, 1)

    def give(d):
        for n, tile in enumerate(back((y + d) % ny * 2 + 1 - core)):
            sa[d, n] = tile
        to_core(d).start()

    def chip_sum(d):
        tiles = back((y + d) % ny * 2 + core)
        to_core(d).wait_recv()
        return [tile + ra[d, n] for n, tile in enumerate(tiles)]

    def give_on(which, ds):
        @pl.when(core == which)
        def _():
            for d in ds:
                give(d)

    give(2)
    for peer in family:
        pltpu.make_async_remote_copy(
            wt.at[dp], wt.at[dp], wt_sem.at[0], wt_sem.at[1],
            device_id=peer, device_id_type=MESH,
        ).start()
    give_on(1, (1, 3, 0))
    tiles = chip_sum(2)
    send(0, tiles[:half])
    send(3, tiles[half:])
    give_on(0, (1, 3, 0))
    ahead = chip_sum(1)
    send(1, ahead[half:])
    for n in range(half):
        kept[0, n] = ahead[n]
    behind = chip_sum(3)
    send(4, behind[:half])
    for n in range(half):
        kept[1, n] = behind[half + n]
    for p in range(2):
        for i, came, goes in ((0, 0, 2), (1, 3, 5)):
            piece = [kept[i, p * half // 2 + n] for n in range(half // 2)]
            send_piece(goes, p, plus_piece(piece, came, p))
    tiles = chip_sum(0)

    scores = sc[...] - jnp.concatenate([lse] * T, axis=0)
    for t in range(T):
        for q in range(N // LANES):
            logp[pl.ds(q * T + t, K, stride=T * N // LANES)] = scores[
                t * K : t * K + K, q * LANES : (q + 1) * LANES
            ]

    tiles = plus(tiles[:half], 4) + plus(tiles[half:], 1)
    tiles = plus(tiles[:half], 2) + plus(tiles[half:], 5)
    family_rows = wt.at[pl.ds(0, len(family))]
    pltpu.make_async_copy(family_rows, family_rows, wt_sem.at[1]).wait()
    weight_row = jnp.sum(wt[...], axis=0) + 1.0
    parts = []
    for j in range(4):
        parts.append(
            jnp.concatenate(
                [tiles[c * half + t * 4 + j] for t in range(T) for c in range(chunks)], axis=0
            )
        )
    lane = lax.broadcasted_iota(jnp.int32, parts[0].shape, 1)
    ends = jnp.where(lane == 0, edge, scale)
    u = mm3(jnp.concatenate([parts[0] * ends, parts[1] * ends], axis=1), ft[0], ft[1], 1)
    v = mm3(jnp.concatenate([parts[2] * scale, parts[3] * scale], axis=1), ft[2], ft[3], 1)
    owned = pl.ds(pl.multiple_of(dp * share, 8), share)
    for t in range(T):
        rows = slice(t * share, (t + 1) * share)
        weight = weight_row[:, t : t + 1]
        new[t, :, :H] = (u[rows] + v[rows] + sl[t, owned, :H]) / weight
        new[t, :, H:] = (u[rows] - v[rows] + sl[t, owned, H:]) / weight

    wait_rows(ls, len(mine), ls_sem.at[0])

    @pl.when(lower)
    def _():
        wait_rows(ls, 3, fin_sem.at[0])

    @pl.when(jnp.logical_not(lower))
    def _():
        wait_rows(ls, 1, ls_sem.at[0])

    pltpu.make_async_copy(family_rows, family_rows, wt_sem.at[0]).wait()
    for d in order:
        to_core(d).wait_send()
    for n in range(6):
        for p in range(2):
            to_chip(n, p).wait_send()


def hand_over(logp, new, logp_out, new_out, sem):
    copies = [
        pltpu.make_async_copy(logp, logp_out, sem.at[0]),
        pltpu.make_async_copy(new, new_out, sem.at[1]),
    ]
    for copy in copies:
        copy.start()
    for copy in copies:
        copy.wait()


def on_device(nx, frames, slices):
    K, R, N = frames.shape
    T = slices.shape[0]
    ny, nz = lax.axis_size("dp") // 2, lax.axis_size("rot") // nx
    assert ny == 4 and R // (2 * ny) == 16
    share = R // (2 * ny)
    body = T * 4 * (share // 8)
    forward = packed_tables(N)
    hbm = pl.BlockSpec(memory_space=pltpu.HBM)
    vmem = pl.BlockSpec(memory_space=pltpu.VMEM)
    dma = pltpu.SemaphoreType.DMA
    logp, new = pl.pallas_call(
        functools.partial(kernel, nx),
        out_shape=(
            jax.ShapeDtypeStruct((K * T * N // LANES, LANES), F32),
            jax.ShapeDtypeStruct((T, share, N), F32),
        ),
        in_specs=[hbm] * 3,
        out_specs=(vmem, vmem),
        scratch_shapes=[
            pltpu.VMEM((K, R, N), jnp.int32),
            pltpu.VMEM((T, R, N), F32),
            pltpu.VMEM((4, N // 2, N // 2), BF16),
            pltpu.VMEM((K, 6, R, LANES), F32),
            pltpu.VMEM((T, 6, R, LANES), F32),
            pltpu.VMEM((6, 8 * T * K, LANES), F32),
            pltpu.VMEM((6, T * K, LANES), F32),
            pltpu.VMEM((T * K, N), F32),
            pltpu.VMEM((nx * nz, 1, LANES), F32),
            pltpu.VMEM((1, 1, LANES), F32),
            pltpu.VMEM((2 * ny, 1, LANES), F32),
            pltpu.VMEM((2, body // 2, 8, LANES), F32),
            pltpu.VMEM((ny, body, 8, LANES), F32),
            pltpu.VMEM((ny, body, 8, LANES), F32),
            pltpu.VMEM((6, body // 2, 8, LANES), F32),
            pltpu.VMEM((6, body // 2, 8, LANES), F32),
            dma((K // GROUP,)),
            dma((2,)),
            dma((3,)),
            dma((2,)),
            dma((2,)),
            dma((ny,)),
            dma((ny,)),
            dma((12,)),
            dma((12,)),
        ],
        compiler_params=pltpu.CompilerParams(
            collective_id=0, has_side_effects=True, vmem_limit_bytes=32 << 20
        ),
    )(*(pltpu.with_memory_space_constraint(v, pltpu.HBM) for v in (frames, slices, jnp.asarray(forward))))
    logp, new = pl.pallas_call(
        hand_over,
        out_shape=(
            jax.ShapeDtypeStruct(logp.shape, F32),
            jax.ShapeDtypeStruct(new.shape, F32),
        ),
        in_specs=[vmem, vmem],
        out_specs=(hbm, hbm),
        scratch_shapes=[dma((2,))],
        compiler_params=pltpu.CompilerParams(vmem_limit_bytes=1 << 20),
    )(logp, new)
    log_resp = logp.reshape(K, N // LANES, T, LANES).transpose(0, 2, 1, 3).reshape(K, T, N)
    return log_resp, new


def solution(mesh, nx=4):
    in_specs = (P("dp", None, None), P("rot", None, None))
    out_specs = (P("dp", "rot", None), P("rot", "dp", None))
    return jax.shard_map(
        functools.partial(on_device, nx),
        mesh=mesh, in_specs=in_specs, out_specs=out_specs, check_vma=False,
    )
```
